768 devices in a mesh: dp: 24 (over z, core), row: 16 (over x, y_lo), col: 2 (over y_hi).
Axes of the slice: x: 4, y: 8 (y_hi: 2, y_lo: 4; y = y_hi * 4 + y_lo), z: 12, core: 2. Of those that a mesh axis runs over, the one named last changes fastest.
Arguments:
- inputs: bfloat16 [98304, 4608], P(('dp', 'col'), 'row'), may hold values from -6 to 6
- grad_keys: bfloat16 [98304, 1024], P(('dp', 'row'), 'col'), may hold values from -6 to 6
- kv_weight: bfloat16 [4608, 1024], P('row', 'col'), may hold values from -0.09375 to 0.09375
Outputs:
- grad_inputs: bfloat16 [98304, 4608], P(('dp', 'col'), 'row')
- grad_weight: bfloat16 [4608, 1024], P(('row', 'dp'), 'col')
The draws below stay inside these ranges and needn't reach their ends.
All inputs are finite; a program needn't handle non-finite values.
Results may differ from the reference program's by a relative error of at most 0.0051.
Values may be sent and summed in bfloat16 or wider, within the bound.
A program may use at most 32 MiB of HBM per device.

```python
import jax
import jax.numpy as jnp
from jax import lax

D = 4608
KVW = 1024
TOKENS = 98304
N_COL = 2


def with_spikes(entries, stream_key, source, target, blocks, factor):
    def block_of(dim):
        return (jnp.arange(entries.shape[dim]) // (entries.shape[dim] // blocks)).reshape((-1,) + (1,) * (entries.ndim - 1 - dim))

    first = jax.random.permutation(stream_key, blocks)[block_of(target)]
    second = (block_of(target) + blocks // 2) % blocks
    return jnp.where((block_of(source) == first) | (block_of(source) == second), factor * entries, entries)


def shard_levels(own_key, extent, cuts, smallest, top_value):
    factor_of = 1.0
    for position, parts in cuts:
        draws = jax.random.uniform(jax.random.fold_in(jax.random.fold_in(own_key, 6), position), (parts,), jnp.float32, smallest / len(cuts), top_value / len(cuts))
        factor_of = factor_of * jnp.repeat(jnp.exp(draws), extent[position] // parts).reshape((-1,) + (1,) * (len(extent) - 1 - position))
    return factor_of


def normal_values(stream_key, dims, scale, bound, split=(), dtype=jnp.bfloat16):
    result = jax.random.normal(stream_key, dims, jnp.float32) * scale
    if len(split) > 0:
        result = shard_levels(stream_key, dims, split, -0.22, 0.18) * result
    return jnp.clip(result, min=-bound, max=bound).astype(dtype)


def gaussian_with(stream_key, shape, scale, limit, shards, heavy, held_as=jnp.bfloat16):
    entries = scale * jax.random.normal(stream_key, shape, jnp.float32)
    if shards:
        entries = entries * shard_levels(stream_key, shape, shards, -0.22, 0.18)
    return jnp.clip(with_spikes(entries, jax.random.fold_in(stream_key, 3), *heavy), -limit, limit).astype(held_as)


def setup_inputs(seed: int = 0) -> dict:
    keys = jax.random.split(jax.random.key(seed), 4)
    inputs = gaussian_with(keys[0], (TOKENS, D), 1.0, 6.0, ((0, 48), (1, 16)), (0, 1, 48, 3.25))
    grad_keys = normal_values(keys[1], (TOKENS, KVW), 1.0, 6.0, ((0, 384), (1, 2)))
    kv_weight = normal_values(keys[2], (D, KVW), D ** -0.5, 0.09375, ((0, 16), (1, 2)))
    return {"inputs": inputs, "grad_keys": grad_keys, "kv_weight": kv_weight}


def rounded(value):
    return lax.optimization_barrier(value.astype(jnp.bfloat16)).astype(jnp.float32)


def reference(inputs, grad_keys, kv_weight):
    half_width = KVW // N_COL
    input_sum = jnp.zeros((TOKENS, D), jnp.float32)
    for column in range(N_COL):
        lower = column * half_width
        upper = lower + half_width
        term = jnp.dot(grad_keys[:, lower:upper], kv_weight[:, lower:upper].T, preferred_element_type=jnp.float32)
        input_sum = input_sum + rounded(term)
    grad_inputs = input_sum.astype(jnp.bfloat16)
    weight_sum = jnp.dot(inputs.T, grad_keys, preferred_element_type=jnp.float32)
    norm_factor = jnp.float32(TOKENS) ** -0.5
    grad_weight = (weight_sum * norm_factor).astype(jnp.bfloat16)
    return grad_inputs, grad_weight
```

```python
import functools

import jax
import jax.numpy as jnp
from jax import lax
from jax.experimental import pallas as pl
from jax.experimental.pallas import tpu as pltpu
from jax.sharding import PartitionSpec as P

MESH = pl.DeviceIdType.MESH
PASSES = 2
LINE = 4
Z = 12


def dot_rows(a, b):
    return lax.dot_general(a, b, (((1,), (0,)), ((), ())), preferred_element_type=jnp.float32)


def dot_last(a, b):
    return lax.dot_general(a, b, (((1,), (1,)), ((), ())), preferred_element_type=jnp.float32)


def kernel(
    norm, xt_hbm, gk_hbm, w_hbm, gi_hbm, gw_out,
    blocks, xs, w_own, w_far, acc, sib, z_send, z_recv, sums, near_in, far_in, gi_tiles,
    local_sem, send_sem, block_sem, w_sem, sib_sem, z_sem, fin_sem,
):
    rows, cols = gk_hbm.shape[0], gk_hbm.shape[1] // PASSES
    feats = w_hbm.shape[0]
    part = feats // Z
    dp, row, p = lax.axis_index("dp"), lax.axis_index("row"), lax.axis_index("col")
    z, core = dp // 2, dp % 2
    x, v = row // LINE, row % LINE
    u = (x + LINE - 2 * p) % LINE
    far = u // 2
    sibling = {"dp": 2 * z + 1 - core}
    partner = {"col": 1 - p}
    x_up = {"row": ((x + 1) % LINE) * LINE + v}
    x_down = {"row": ((x + LINE - 1) % LINE) * LINE + v}
    y_up, y_down = {"row": row + 1}, {"row": row - 1}

    started = []
    sends = iter(range(10_000))

    def send(src, dst, recv, device, when=None):
        copy = pltpu.make_async_remote_copy(
            src_ref=src, dst_ref=dst, send_sem=send_sem.at[next(sends)], recv_sem=recv,
            device_id=device, device_id_type=MESH,
        )
        started.append((copy, when))
        if when is None:
            copy.start()
        else:
            pl.when(when)(copy.start)

    def arrived(dst, recv, device, when=None):
        copy = pltpu.make_async_remote_copy(
            src_ref=dst, dst_ref=dst, send_sem=send_sem.at[0], recv_sem=recv,
            device_id=device, device_id_type=MESH,
        )
        if when is None:
            copy.wait_recv()
        else:
            pl.when(when)(copy.wait_recv)

    def order(line_far, k):
        upper = v // 2
        mirrored = v + upper * (3 - 2 * v)
        near_k = (mirrored, 1 - mirrored, 2, 3)[k]
        far_k = (3, 2, 0, 1)[k]
        low = line_far * far_k + (1 - line_far) * near_k
        return low + upper * (3 - 2 * low)

    def column_slot(uu, k):
        ff = uu // 2
        return ff * (20 - 4 * uu) + (1 - ff) * 4 * uu + order(ff, k)

    def half(s, slot, i):
        return blocks.at[s, slot, pl.ds(i * (rows // 2), rows // 2)]

    def accumulate(s, slot):
        h, t = slot // 8, slot % 8
        acc[s, h] += dot_rows(xs[t], blocks[s, slot])

    own_slot = 4 * u + v
    own = [
        pltpu.make_async_copy(gk_hbm.at[:, pl.ds(s * cols, cols)], blocks.at[s, own_slot], local_sem.at[s])
        for s in range(PASSES)
    ]
    tiles = xs.shape[0]
    loads = [
        pltpu.make_async_copy(xt_hbm.at[:, pl.ds(t * rows, rows)], xs.at[t], local_sem.at[PASSES + t])
        for t in range(tiles)
    ]
    load_w = pltpu.make_async_copy(w_hbm, w_own, local_sem.at[PASSES + tiles])
    is_near, is_far = far == 0, far == 1
    for copy in own:
        pl.when(is_near)(copy.start)

    far_u = u - 2
    far_x = (3 - far_u + 2 * (1 - p)) % LINE
    far_entry = 3 * (1 - v // 2)
    far_device = {"row": far_x * LINE + far_entry, "col": 1 - p}
    far_slot = 8 + 4 * far_u + v

    def start_far(s):
        send(
            gk_hbm.at[:, pl.ds(s * cols, cols)], blocks.at[s, far_slot], block_sem.at[s, far_slot, 0],
            far_device, is_far,
        )

    def column_step(s, k, first):
        j = order(far, k)
        slot = column_slot(u, k)
        here, sem = blocks.at[s, slot], block_sem.at[s, slot, 0]
        entry = far * 3 * (1 - j // 2) + (1 - far) * j
        if first:
            if k == 0:
                pl.when(is_near)(own[s].wait)
                arrived(here, sem, sibling, is_far)
            else:
                arrived(here, sem, sibling)
        send(here, here, sem, x_up)
        send(here, here, sem, x_down)
        send(here, here, sem, y_down, jnp.logical_and(v <= entry, v > 0))
        send(here, here, sem, y_up, jnp.logical_and(v >= entry, v < LINE - 1))

    def side_step(s, k):
        left = column_slot((u + LINE - 1) % LINE, k)
        right = column_slot((u + 1) % LINE, k)
        arrived(blocks.at[s, left], block_sem.at[s, left, 0], sibling)
        send(half(s, left, 0), half(s, left, 0), block_sem.at[s, left, 0], x_up)
        arrived(blocks.at[s, right], block_sem.at[s, right, 0], sibling)
        send(half(s, right, 1), half(s, right, 1), block_sem.at[s, right, 1], x_down)
        accumulate(s, left)
        accumulate(s, right)

    def opposite_step(s, k):
        slot = column_slot((u + 2) % LINE, k)
        for i in range(2):
            arrived(half(s, slot, i), block_sem.at[s, slot, i], sibling)
        accumulate(s, slot)

    def cores_start(s):
        send(acc.at[s, 1 - core], sib.at[s], sib_sem.at[s], sibling)

    def z_start(s):
        arrived(sib.at[s], sib_sem.at[s], sibling)
        acc[s, core] += sib[s]
        for zz in range(Z):
            z_send[s, zz] = acc[s, core, pl.ds(zz * part, part)].astype(jnp.bfloat16)
        for d in range(1, Z):
            to = (z + d) % Z
            send(z_send.at[s, to], z_recv.at[s, z], z_sem.at[s, z], {"dp": 2 * to + core})

    def z_finish(s):
        total = acc[s, core, pl.ds(pl.multiple_of(z * part, 8), part)]
        for d in range(1, Z):
            source = (z + Z - d) % Z
            arrived(z_recv.at[s, source], z_sem.at[s, source], sibling)
            total = total + z_recv[s, source].astype(jnp.float32)
        for i in range(2):
            sums[i, :, s * cols:(s + 1) * cols] = total[i * (part // 2):(i + 1) * (part // 2)]

    w_rows = feats // 2
    w_part = w_far.at[pl.ds(pl.multiple_of(core * w_rows, 16), w_rows)]
    w_other = w_far.at[pl.ds(pl.multiple_of((1 - core) * w_rows, 16), w_rows)]

    start_far(0)
    for copy in loads:
        copy.start()
    load_w.start()
    acc[...] = jnp.zeros_like(acc)
    for s in range(PASSES):
        for k in range(LINE):
            column_step(s, k, True)
            if s == 0 and k == 0:
                start_far(1)
                send(w_hbm.at[pl.ds(pl.multiple_of(core * w_rows, 16), w_rows)], w_part, w_sem.at[0], partner)
                for copy in loads:
                    copy.wait()
            side_step(s, k)
            accumulate(s, column_slot(u, k))
            if s == 1 and k == 0:
                z_start(0)
            if s == 0 and k == 3:
                arrived(w_part, w_sem.at[0], sibling)
                send(w_part, w_part, w_sem.at[1], sibling)
            if k > 0:
                opposite_step(s, k - 1)
        opposite_step(s, LINE - 1)
        cores_start(s)
    z_finish(0)
    load_w.wait()
    arrived(w_other, w_sem.at[1], sibling)
    z_start(1)

    def tile(t, carry):
        def term(weight, slot):
            total = dot_last(weight[:, :cols], blocks[0, slot])
            for s in range(1, PASSES):
                total = total + dot_last(weight[:, s * cols:(s + 1) * cols], blocks[s, slot])
            return total.astype(jnp.bfloat16).astype(jnp.float32)

        gi_tiles[t] = (term(w_own, t) + term(w_far, t + 8)).astype(jnp.bfloat16)
        return carry

    lax.fori_loop(0, tiles, tile, 0)
    stores = [
        pltpu.make_async_copy(gi_tiles.at[t], gi_hbm.at[:, pl.ds(t * rows, rows)], local_sem.at[t])
        for t in range(tiles)
    ]
    for copy in stores:
        copy.start()

    z_finish(1)
    is_zero, is_one = core == 0, core == 1
    send(sums.at[1], near_in, fin_sem.at[0], sibling, is_zero)
    send(sums.at[0], far_in, fin_sem.at[1], {"dp": 2 * z, "col": 1 - p}, is_one)
    send(sums.at[1], far_in, fin_sem.at[1], {"dp": 2 * z + 1, "col": 1 - p}, is_one)

    arrived(far_in, fin_sem.at[1], sibling)

    @pl.when(is_zero)
    def _():
        gw_out[...] = ((sums[0] + far_in[...]) * norm).astype(jnp.bfloat16)

    @pl.when(is_one)
    def _():
        arrived(near_in, fin_sem.at[0], sibling)
        gw_out[...] = ((near_in[...] + far_in[...]) * norm).astype(jnp.bfloat16)

    for copy in stores:
        copy.wait()
    for copy, when in started:
        if when is None:
            copy.wait_send()
        else:
            pl.when(when)(copy.wait_send)


def per_device(inputs, grad_keys, kv_weight):
    tokens, feats = inputs.shape
    rows, width = grad_keys.shape
    cols = width // PASSES
    tiles = tokens // rows
    replicas = lax.axis_size("dp")
    part = feats // Z
    norm = float(tokens * lax.axis_size("col") * replicas) ** (-0.5)
    bf16, f32 = jnp.bfloat16, jnp.float32
    hbm = pl.BlockSpec(memory_space=pl.ANY)
    gi, gw = pl.pallas_call(
        functools.partial(kernel, norm),
        out_shape=(
            jax.ShapeDtypeStruct((feats, tokens), bf16),
            jax.ShapeDtypeStruct((feats // replicas, width), bf16),
        ),
        in_specs=[hbm] * 3,
        out_specs=(hbm, pl.BlockSpec(memory_space=pltpu.VMEM)),
        scratch_shapes=[
            pltpu.VMEM((PASSES, 16, rows, cols), bf16),
            pltpu.VMEM((tiles, feats, rows), bf16),
            pltpu.VMEM((feats, width), bf16),
            pltpu.VMEM((feats, width), bf16),
            pltpu.VMEM((PASSES, 2, feats, cols), f32),
            pltpu.VMEM((PASSES, feats, cols), f32),
            pltpu.VMEM((PASSES, Z, part, cols), bf16),
            pltpu.VMEM((PASSES, Z, part, cols), bf16),
            pltpu.VMEM((2, part // 2, width), f32),
            pltpu.VMEM((part // 2, width), f32),
            pltpu.VMEM((part // 2, width), f32),
            pltpu.VMEM((tiles, feats, rows), bf16),
            pltpu.SemaphoreType.DMA((PASSES + tiles + 1,)),
            pltpu.SemaphoreType.DMA((96,)),
            pltpu.SemaphoreType.DMA((PASSES, 16, 2)),
            pltpu.SemaphoreType.DMA((2,)),
            pltpu.SemaphoreType.DMA((PASSES,)),
            pltpu.SemaphoreType.DMA((PASSES, Z)),
            pltpu.SemaphoreType.DMA((2,)),
        ],
        compiler_params=pltpu.CompilerParams(has_side_effects=True),
    )(inputs.T, grad_keys, kv_weight)
    return gi.T, gw


def solution(mesh):
    in_specs = (P(("dp", "col"), "row"), P(("dp", "row"), "col"), P("row", "col"))
    out_specs = (P(("dp", "col"), "row"), P(("row", "dp"), "col"))
    return jax.shard_map(
        per_device, mesh=mesh, in_specs=in_specs, out_specs=out_specs, check_vma=False
    )
```

```python
import functools

import jax
import jax.numpy as jnp
from jax import lax
from jax.experimental import pallas as pl
from jax.experimental.pallas import tpu as pltpu
from jax.sharding import PartitionSpec as P


def gather_program():
    program = [("F", s) for s in range(2)]
    for i in range(12):
        if i < 8:
            program.append(("Y", i))
        if i == 0:
            program.append(("W", 0))
        if i < 8:
            program.append(("X", i))
        if 2 <= i < 10:
            program += [("L", i - 2), ("R", i - 2)]
        if i == 4:
            program.append(("V", 0))
        if i >= 4:
            program.append(("O", i - 4))
        if i == 7:
            program.append(("C", 0))
        if i == 9:
            program.append(("Z", 0))
    return program + [("C", 1), ("E", 0)]


PROGRAM = gather_program()
MESH = pl.DeviceIdType.MESH
PASSES = 2
LINE = 4
Z = 12


def dot_rows(a, b):
    return lax.dot_general(a, b, (((1,), (0,)), ((), ())), preferred_element_type=jnp.float32)


def dot_last(a, b):
    return lax.dot_general(a, b, (((1,), (1,)), ((), ())), preferred_element_type=jnp.float32)


def kernel(
    norm, xt_hbm, gk_hbm, w_hbm, gi_hbm, gw_out,
    blocks, xs, w_own, w_far, acc, sib, z_send, z_recv, sums, near_in, far_in, gi_tiles,
    local_sem, send_sem, block_sem, w_sem, sib_sem, z_sem, fin_sem,
):
    rows, cols = gk_hbm.shape[0], gk_hbm.shape[1] // PASSES
    feats = w_hbm.shape[0]
    part = feats // Z
    dp, row, p = lax.axis_index("dp"), lax.axis_index("row"), lax.axis_index("col")
    z, core = dp // 2, dp % 2
    x, v = row // LINE, row % LINE
    u = (x + LINE - 2 * p) % LINE
    far = u // 2
    sibling = {"dp": 2 * z + 1 - core}
    partner = {"col": 1 - p}
    x_up = {"row": ((x + 1) % LINE) * LINE + v}
    x_down = {"row": ((x + LINE - 1) % LINE) * LINE + v}
    y_up, y_down = {"row": row + 1}, {"row": row - 1}

    started = []
    sends = iter(range(10_000))

    def send(src, dst, recv, device, when=None):
        copy = pltpu.make_async_remote_copy(
            src_ref=src, dst_ref=dst, send_sem=send_sem.at[next(sends)], recv_sem=recv,
            device_id=device, device_id_type=MESH,
        )
        started.append((copy, when))
        if when is None:
            copy.start()
        else:
            pl.when(when)(copy.start)

    def arrived(dst, recv, device, when=None):
        copy = pltpu.make_async_remote_copy(
            src_ref=dst, dst_ref=dst, send_sem=send_sem.at[0], recv_sem=recv,
            device_id=device, device_id_type=MESH,
        )
        if when is None:
            copy.wait_recv()
        else:
            pl.when(when)(copy.wait_recv)

    def order(line_far, k):
        upper = v // 2
        mirrored = v + upper * (3 - 2 * v)
        near_k = (mirrored, 1 - mirrored, 2, 3)[k]
        far_k = (3, 2, 0, 1)[k]
        low = line_far * far_k + (1 - line_far) * near_k
        return low + upper * (3 - 2 * low)

    def column_slot(uu, k):
        ff = uu // 2
        return ff * (20 - 4 * uu) + (1 - ff) * 4 * uu + order(ff, k)

    def half(s, slot, i):
        return blocks.at[s, slot, pl.ds(i * (rows // 2), rows // 2)]

    def accumulate(s, slot):
        h, t = slot // 8, slot % 8
        acc[s, h] += dot_rows(xs[t], blocks[s, slot])

    own_slot = 4 * u + v
    own = [
        pltpu.make_async_copy(gk_hbm.at[:, pl.ds(s * cols, cols)], blocks.at[s, own_slot], local_sem.at[s])
        for s in range(PASSES)
    ]
    tiles = xs.shape[0]
    loads = [
        pltpu.make_async_copy(xt_hbm.at[:, pl.ds(t * rows, rows)], xs.at[t], local_sem.at[PASSES + t])
        for t in range(tiles)
    ]
    load_w = pltpu.make_async_copy(w_hbm, w_own, local_sem.at[PASSES + tiles])
    is_near, is_far = far == 0, far == 1
    for copy in own:
        pl.when(is_near)(copy.start)

    far_u = u - 2
    far_x = (3 - far_u + 2 * (1 - p)) % LINE
    far_entry = 3 * (1 - v // 2)
    far_device = {"row": far_x * LINE + far_entry, "col": 1 - p}
    far_slot = 8 + 4 * far_u + v

    def start_far(s):
        send(
            gk_hbm.at[:, pl.ds(s * cols, cols)], blocks.at[s, far_slot], block_sem.at[s, far_slot, 0],
            far_device, is_far,
        )

    def line_step(s, k):
        j = order(far, k)
        slot = column_slot(u, k)
        here, sem = blocks.at[s, slot], block_sem.at[s, slot, 0]
        entry = far * 3 * (1 - j // 2) + (1 - far) * j
        if k == 0:
            pl.when(is_near)(own[s].wait)
            arrived(here, sem, sibling, is_far)
        else:
            arrived(here, sem, sibling)
        send(here, here, sem, y_down, jnp.logical_and(v <= entry, v > 0))
        send(here, here, sem, y_up, jnp.logical_and(v >= entry, v < LINE - 1))

    def ring_step(s, k):
        slot = column_slot(u, k)
        here, sem = blocks.at[s, slot], block_sem.at[s, slot, 0]
        send(here, here, sem, x_up)
        send(here, here, sem, x_down)
        accumulate(s, slot)

    def left_step(s, k):
        slot = column_slot((u + LINE - 1) % LINE, k)
        arrived(blocks.at[s, slot], block_sem.at[s, slot, 0], sibling)
        send(half(s, slot, 0), half(s, slot, 0), block_sem.at[s, slot, 0], x_up)
        accumulate(s, slot)

    def right_step(s, k):
        slot = column_slot((u + 1) % LINE, k)
        arrived(blocks.at[s, slot], block_sem.at[s, slot, 0], sibling)
        send(half(s, slot, 1), half(s, slot, 1), block_sem.at[s, slot, 1], x_down)
        accumulate(s, slot)

    def opposite_step(s, k):
        slot = column_slot((u + 2) % LINE, k)
        for i in range(2):
            arrived(half(s, slot, i), block_sem.at[s, slot, i], sibling)
        accumulate(s, slot)

    def cores_start(s):
        send(acc.at[s, 1 - core], sib.at[s], sib_sem.at[s], sibling)

    def z_start(s):
        arrived(sib.at[s], sib_sem.at[s], sibling)
        acc[s, core] += sib[s]
        for zz in range(Z):
            z_send[s, zz] = acc[s, core, pl.ds(zz * part, part)].astype(jnp.bfloat16)
        for d in range(1, Z):
            to = (z + d) % Z
            send(z_send.at[s, to], z_recv.at[s, z], z_sem.at[s, z], {"dp": 2 * to + core})

    def z_finish(s):
        total = acc[s, core, pl.ds(pl.multiple_of(z * part, 8), part)]
        for d in range(1, Z):
            source = (z + Z - d) % Z
            arrived(z_recv.at[s, source], z_sem.at[s, source], sibling)
            total = total + z_recv[s, source].astype(jnp.float32)
        for i in range(2):
            sums[i, :, s * cols:(s + 1) * cols] = total[i * (part // 2):(i + 1) * (part // 2)]

    w_rows = feats // 2
    w_part = w_far.at[pl.ds(pl.multiple_of(core * w_rows, 16), w_rows)]
    w_other = w_far.at[pl.ds(pl.multiple_of((1 - core) * w_rows, 16), w_rows)]

    barrier = pltpu.get_barrier_semaphore()

    def greet(device, when=None):
        def signal():
            pl.semaphore_signal(barrier, inc=1, device_id=device, device_id_type=MESH)

        if when is None:
            signal()
        else:
            pl.when(when)(signal)

    greet(x_up)
    greet(x_down)
    greet(sibling)
    for k in range(2):
        greet({"dp": 2 * z + k, "col": 1 - p})
    for step in (1, 7):
        y = (4 * p + v + step) % 8
        greet({"row": x * LINE + y % LINE, "col": y // LINE})
    for d in range(1, Z):
        greet({"dp": 2 * ((z + d) % Z) + core})
    far_greets = jnp.logical_and(is_far, v % 3 == 0)
    for i in range(2):
        source_x = (5 - u + 2 * (1 - p)) % LINE
        greet({"row": source_x * LINE + 2 * (1 - v // 3) + i, "col": 1 - p}, far_greets)

    for copy in loads:
        copy.start()
    load_w.start()
    acc[...] = jnp.zeros_like(acc)
    pl.semaphore_wait(barrier, 18 + far)
    def weight_send():
        send(w_hbm.at[pl.ds(pl.multiple_of(core * w_rows, 16), w_rows)], w_part, w_sem.at[0], partner)
        for copy in loads:
            copy.wait()

    def weight_forward():
        arrived(w_part, w_sem.at[0], sibling)
        send(w_part, w_part, w_sem.at[1], sibling)

    steps = dict(
        F=lambda i: start_far(i), W=lambda i: weight_send(), V=lambda i: weight_forward(),
        Y=lambda i: line_step(*divmod(i, LINE)), X=lambda i: ring_step(*divmod(i, LINE)),
        L=lambda i: left_step(*divmod(i, LINE)), R=lambda i: right_step(*divmod(i, LINE)),
        O=lambda i: opposite_step(*divmod(i, LINE)),
        C=cores_start, Z=z_start, E=z_finish,
    )
    for name, i in PROGRAM:
        steps[name](i)
    load_w.wait()
    arrived(w_other, w_sem.at[1], sibling)
    z_start(1)

    def tile(t, carry):
        def term(weight, slot):
            total = dot_last(weight[:, :cols], blocks[0, slot])
            for s in range(1, PASSES):
                total = total + dot_last(weight[:, s * cols:(s + 1) * cols], blocks[s, slot])
            return total.astype(jnp.bfloat16).astype(jnp.float32)

        gi_tiles[t] = (term(w_own, t) + term(w_far, t + 8)).astype(jnp.bfloat16)
        return carry

    lax.fori_loop(0, tiles, tile, 0)
    stores = [
        pltpu.make_async_copy(gi_tiles.at[t], gi_hbm.at[:, pl.ds(t * rows, rows)], local_sem.at[t])
        for t in range(tiles)
    ]
    for copy in stores:
        copy.start()

    z_finish(1)
    is_zero, is_one = core == 0, core == 1
    send(sums.at[1], near_in, fin_sem.at[0], sibling, is_zero)
    send(sums.at[0], far_in, fin_sem.at[1], {"dp": 2 * z, "col": 1 - p}, is_one)
    send(sums.at[1], far_in, fin_sem.at[1], {"dp": 2 * z + 1, "col": 1 - p}, is_one)

    arrived(far_in, fin_sem.at[1], sibling)

    @pl.when(is_zero)
    def _():
        gw_out[...] = ((sums[0] + far_in[...]) * norm).astype(jnp.bfloat16)

    @pl.when(is_one)
    def _():
        arrived(near_in, fin_sem.at[0], sibling)
        gw_out[...] = ((near_in[...] + far_in[...]) * norm).astype(jnp.bfloat16)

    for copy in stores:
        copy.wait()
    for copy, when in started:
        if when is None:
            copy.wait_send()
        else:
            pl.when(when)(copy.wait_send)


def per_device(inputs, grad_keys, kv_weight):
    tokens, feats = inputs.shape
    rows, width = grad_keys.shape
    cols = width // PASSES
    tiles = tokens // rows
    replicas = lax.axis_size("dp")
    part = feats // Z
    norm = float(tokens * lax.axis_size("col") * replicas) ** (-0.5)
    bf16, f32 = jnp.bfloat16, jnp.float32
    hbm = pl.BlockSpec(memory_space=pl.ANY)
    gi, gw = pl.pallas_call(
        functools.partial(kernel, norm),
        out_shape=(
            jax.ShapeDtypeStruct((feats, tokens), bf16),
            jax.ShapeDtypeStruct((feats // replicas, width), bf16),
        ),
        in_specs=[hbm] * 3,
        out_specs=(hbm, pl.BlockSpec(memory_space=pltpu.VMEM)),
        scratch_shapes=[
            pltpu.VMEM((PASSES, 16, rows, cols), bf16),
            pltpu.VMEM((tiles, feats, rows), bf16),
            pltpu.VMEM((feats, width), bf16),
            pltpu.VMEM((feats, width), bf16),
            pltpu.VMEM((PASSES, 2, feats, cols), f32),
            pltpu.VMEM((PASSES, feats, cols), f32),
            pltpu.VMEM((PASSES, Z, part, cols), bf16),
            pltpu.VMEM((PASSES, Z, part, cols), bf16),
            pltpu.VMEM((2, part // 2, width), f32),
            pltpu.VMEM((part // 2, width), f32),
            pltpu.VMEM((part // 2, width), f32),
            pltpu.VMEM((tiles, feats, rows), bf16),
            pltpu.SemaphoreType.DMA((PASSES + tiles + 1,)),
            pltpu.SemaphoreType.DMA((96,)),
            pltpu.SemaphoreType.DMA((PASSES, 16, 2)),
            pltpu.SemaphoreType.DMA((2,)),
            pltpu.SemaphoreType.DMA((PASSES,)),
            pltpu.SemaphoreType.DMA((PASSES, Z)),
            pltpu.SemaphoreType.DMA((2,)),
        ],
        compiler_params=pltpu.CompilerParams(collective_id=0, has_side_effects=True),
    )(inputs.T, grad_keys, kv_weight)
    return gi.T, gw


def solution(mesh):
    in_specs = (P(("dp", "col"), "row"), P(("dp", "row"), "col"), P("row", "col"))
    out_specs = (P(("dp", "col"), "row"), P(("row", "dp"), "col"))
    return jax.shard_map(
        per_device, mesh=mesh, in_specs=in_specs, out_specs=out_specs, check_vma=False
    )
```

```python
import functools

import jax
import jax.numpy as jnp
from jax import lax
from jax.experimental import pallas as pl
from jax.experimental.pallas import tpu as pltpu
from jax.sharding import PartitionSpec as P


def gather_program():
    program = [("F", s) for s in range(2)]
    for i in range(12):
        if i < 8:
            program.append(("Y", i))
        if i == 0:
            program.append(("W", 0))
        if i < 8:
            program.append(("X", i))
        if 2 <= i < 10:
            program += [("L", i - 2), ("R", i - 2)]
        if 1 <= i <= 6:
            program.append(("T", i))
        if i == 4:
            program.append(("V", 0))
        if i >= 4:
            program.append(("O", i - 4))
        if i == 7:
            program.append(("C", 0))
        if i == 9:
            program.append(("Z", 0))
    return program + [("C", 1), ("E", 0)]


PROGRAM = gather_program()
MESH = pl.DeviceIdType.MESH
PASSES = 2
LINE = 4
Z = 12


def dot_rows(a, b):
    return lax.dot_general(a, b, (((1,), (0,)), ((), ())), preferred_element_type=jnp.float32)


def dot_last(a, b):
    return lax.dot_general(a, b, (((1,), (1,)), ((), ())), preferred_element_type=jnp.float32)


def kernel(
    norm, xt_hbm, gk_hbm, w_hbm, gi_hbm, gw_out,
    blocks, xs, w_own, w_far, acc, sib, z_send, z_recv, sums, near_in, far_in, gi_tiles,
    local_sem, send_sem, block_sem, w_sem, sib_sem, z_sem, fin_sem, token_sem,
):
    rows, cols = gk_hbm.shape[0], gk_hbm.shape[1] // PASSES
    feats = w_hbm.shape[0]
    part = feats // Z
    dp, row, p = lax.axis_index("dp"), lax.axis_index("row"), lax.axis_index("col")
    z, core = dp // 2, dp % 2
    x, v = row // LINE, row % LINE
    u = (x + LINE - 2 * p) % LINE
    far = u // 2
    sibling = {"dp": 2 * z + 1 - core}
    partner = {"col": 1 - p}
    x_up = {"row": ((x + 1) % LINE) * LINE + v}
    x_down = {"row": ((x + LINE - 1) % LINE) * LINE + v}
    y_up, y_down = {"row": row + 1}, {"row": row - 1}

    started = []
    sends = iter(range(10_000))

    def send(src, dst, recv, device, when=None):
        copy = pltpu.make_async_remote_copy(
            src_ref=src, dst_ref=dst, send_sem=send_sem.at[next(sends)], recv_sem=recv,
            device_id=device, device_id_type=MESH,
        )
        started.append((copy, when))
        if when is None:
            copy.start()
        else:
            pl.when(when)(copy.start)

    def arrived(dst, recv, device, when=None):
        copy = pltpu.make_async_remote_copy(
            src_ref=dst, dst_ref=dst, send_sem=send_sem.at[0], recv_sem=recv,
            device_id=device, device_id_type=MESH,
        )
        if when is None:
            copy.wait_recv()
        else:
            pl.when(when)(copy.wait_recv)

    def order(line_far, k):
        upper = v // 2
        mirrored = v + upper * (3 - 2 * v)
        near_k = (mirrored, 1 - mirrored, 2, 3)[k]
        far_k = (3, 2, 0, 1)[k]
        low = line_far * far_k + (1 - line_far) * near_k
        return low + upper * (3 - 2 * low)

    def column_slot(uu, k):
        ff = uu // 2
        return ff * (20 - 4 * uu) + (1 - ff) * 4 * uu + order(ff, k)

    def half(s, slot, i):
        return blocks.at[s, slot, pl.ds(i * (rows // 2), rows // 2)]

    def accumulate(s, slot):
        h, t = slot // 8, slot % 8
        acc[s, h] += dot_rows(xs[t], blocks[s, slot])

    own_slot = 4 * u + v
    own = [
        pltpu.make_async_copy(gk_hbm.at[:, pl.ds(s * cols, cols)], blocks.at[s, own_slot], local_sem.at[s])
        for s in range(PASSES)
    ]
    tiles = xs.shape[0]
    loads = [
        pltpu.make_async_copy(xt_hbm.at[:, pl.ds(t * rows, rows)], xs.at[t], local_sem.at[PASSES + t])
        for t in range(tiles)
    ]
    load_w = pltpu.make_async_copy(w_hbm, w_own, local_sem.at[PASSES + tiles])
    is_near, is_far = far == 0, far == 1
    for copy in own:
        pl.when(is_near)(copy.start)

    far_u = u - 2
    far_x = (3 - far_u + 2 * (1 - p)) % LINE
    far_entry = 3 * (1 - v // 2)
    far_device = {"row": far_x * LINE + far_entry, "col": 1 - p}
    far_slot = 8 + 4 * far_u + v

    def start_far(s):
        send(
            gk_hbm.at[:, pl.ds(s * cols, cols)], blocks.at[s, far_slot], block_sem.at[s, far_slot, 0],
            far_device, is_far,
        )

    def line_step(s, k):
        j = order(far, k)
        slot = column_slot(u, k)
        here, sem = blocks.at[s, slot], block_sem.at[s, slot, 0]
        entry = far * 3 * (1 - j // 2) + (1 - far) * j
        if k == 0:
            pl.when(is_near)(own[s].wait)
            arrived(here, sem, sibling, is_far)
        else:
            arrived(here, sem, sibling)
        send(here, here, sem, y_down, jnp.logical_and(v <= entry, v > 0))
        send(here, here, sem, y_up, jnp.logical_and(v >= entry, v < LINE - 1))

    def ring_step(s, k):
        slot = column_slot(u, k)
        here, sem = blocks.at[s, slot], block_sem.at[s, slot, 0]
        send(here, here, sem, x_up)
        send(here, here, sem, x_down)
        accumulate(s, slot)

    def left_step(s, k):
        slot = column_slot((u + LINE - 1) % LINE, k)
        arrived(blocks.at[s, slot], block_sem.at[s, slot, 0], sibling)
        send(half(s, slot, 0), half(s, slot, 0), block_sem.at[s, slot, 0], x_up)
        accumulate(s, slot)

    def right_step(s, k):
        slot = column_slot((u + 1) % LINE, k)
        arrived(blocks.at[s, slot], block_sem.at[s, slot, 0], sibling)
        send(half(s, slot, 1), half(s, slot, 1), block_sem.at[s, slot, 1], x_down)
        accumulate(s, slot)

    def opposite_step(s, k):
        slot = column_slot((u + 2) % LINE, k)
        for i in range(2):
            arrived(half(s, slot, i), block_sem.at[s, slot, i], sibling)
        accumulate(s, slot)

    def cores_start(s):
        send(acc.at[s, 1 - core], sib.at[s], sib_sem.at[s], sibling)

    def z_start(s):
        arrived(sib.at[s], sib_sem.at[s], sibling)
        acc[s, core] += sib[s]
        for zz in range(Z):
            z_send[s, zz] = acc[s, core, pl.ds(zz * part, part)].astype(jnp.bfloat16)
        for d in range(1, Z):
            to = (z + d) % Z
            send(z_send.at[s, to], z_recv.at[s, z], z_sem.at[s, z], {"dp": 2 * to + core})

    def z_finish(s):
        total = acc[s, core, pl.ds(pl.multiple_of(z * part, 8), part)]
        for d in range(1, Z):
            source = (z + Z - d) % Z
            arrived(z_recv.at[s, source], z_sem.at[s, source], sibling)
            total = total + z_recv[s, source].astype(jnp.float32)
        for i in range(2):
            sums[i, :, s * cols:(s + 1) * cols] = total[i * (part // 2):(i + 1) * (part // 2)]

    w_rows = feats // 2
    w_part = w_far.at[pl.ds(pl.multiple_of(core * w_rows, 16), w_rows)]
    w_other = w_far.at[pl.ds(pl.multiple_of((1 - core) * w_rows, 16), w_rows)]

    barrier = pltpu.get_barrier_semaphore()

    def greet(device, when=None):
        def signal():
            pl.semaphore_signal(barrier, inc=1, device_id=device, device_id_type=MESH)

        if when is None:
            signal()
        else:
            pl.when(when)(signal)

    greet(x_up)
    greet(x_down)
    greet(sibling)
    for k in range(2):
        greet({"dp": 2 * z + k, "col": 1 - p})
    for step in (1, 7):
        y = (4 * p + v + step) % 8
        greet({"row": x * LINE + y % LINE, "col": y // LINE})
    z_up, z_down = {"dp": 2 * ((z + 1) % Z) + core}, {"dp": 2 * ((z + Z - 1) % Z) + core}
    greet(z_up)
    greet(z_down)
    far_greets = jnp.logical_and(is_far, v % 3 == 0)
    for i in range(2):
        source_x = (5 - u + 2 * (1 - p)) % LINE
        greet({"row": source_x * LINE + 2 * (1 - v // 3) + i, "col": 1 - p}, far_greets)

    for copy in loads:
        copy.start()
    load_w.start()
    acc[...] = jnp.zeros_like(acc)
    pl.semaphore_wait(barrier, 9 + far)
    def weight_send():
        send(w_hbm.at[pl.ds(pl.multiple_of(core * w_rows, 16), w_rows)], w_part, w_sem.at[0], partner)
        for copy in loads:
            copy.wait()

    def weight_forward():
        arrived(w_part, w_sem.at[0], sibling)
        send(w_part, w_part, w_sem.at[1], sibling)

    def token_round(r):
        for i, (device, rounds) in enumerate(((z_up, 5), (z_down, 4))):
            if 1 <= r - 1 <= rounds:
                pl.semaphore_wait(token_sem.at[i, r - 1], 1)
            if r <= rounds:
                pl.semaphore_signal(token_sem.at[i, r], inc=1, device_id=device, device_id_type=MESH)

    steps = dict(
        T=token_round,
        F=lambda i: start_far(i), W=lambda i: weight_send(), V=lambda i: weight_forward(),
        Y=lambda i: line_step(*divmod(i, LINE)), X=lambda i: ring_step(*divmod(i, LINE)),
        L=lambda i: left_step(*divmod(i, LINE)), R=lambda i: right_step(*divmod(i, LINE)),
        O=lambda i: opposite_step(*divmod(i, LINE)),
        C=cores_start, Z=z_start, E=z_finish,
    )
    for name, i in PROGRAM:
        steps[name](i)
    load_w.wait()
    arrived(w_other, w_sem.at[1], sibling)
    z_start(1)

    def tile(t, carry):
        def term(weight, slot):
            total = dot_last(weight[:, :cols], blocks[0, slot])
            for s in range(1, PASSES):
                total = total + dot_last(weight[:, s * cols:(s + 1) * cols], blocks[s, slot])
            return total.astype(jnp.bfloat16).astype(jnp.float32)

        gi_tiles[t] = (term(w_own, t) + term(w_far, t + 8)).astype(jnp.bfloat16)
        return carry

    lax.fori_loop(0, tiles, tile, 0)
    stores = [
        pltpu.make_async_copy(gi_tiles.at[t], gi_hbm.at[:, pl.ds(t * rows, rows)], local_sem.at[t])
        for t in range(tiles)
    ]
    for copy in stores:
        copy.start()

    z_finish(1)
    is_zero, is_one = core == 0, core == 1
    send(sums.at[1], near_in, fin_sem.at[0], sibling, is_zero)
    send(sums.at[0], far_in, fin_sem.at[1], {"dp": 2 * z, "col": 1 - p}, is_one)
    send(sums.at[1], far_in, fin_sem.at[1], {"dp": 2 * z + 1, "col": 1 - p}, is_one)

    arrived(far_in, fin_sem.at[1], sibling)

    @pl.when(is_zero)
    def _():
        gw_out[...] = ((sums[0] + far_in[...]) * norm).astype(jnp.bfloat16)

    @pl.when(is_one)
    def _():
        arrived(near_in, fin_sem.at[0], sibling)
        gw_out[...] = ((near_in[...] + far_in[...]) * norm).astype(jnp.bfloat16)

    for copy in stores:
        copy.wait()
    for copy, when in started:
        if when is None:
            copy.wait_send()
        else:
            pl.when(when)(copy.wait_send)


def per_device(inputs, grad_keys, kv_weight):
    tokens, feats = inputs.shape
    rows, width = grad_keys.shape
    cols = width // PASSES
    tiles = tokens // rows
    replicas = lax.axis_size("dp")
    part = feats // Z
    norm = float(tokens * lax.axis_size("col") * replicas) ** (-0.5)
    bf16, f32 = jnp.bfloat16, jnp.float32
    hbm = pl.BlockSpec(memory_space=pl.ANY)
    gi, gw = pl.pallas_call(
        functools.partial(kernel, norm),
        out_shape=(
            jax.ShapeDtypeStruct((feats, tokens), bf16),
            jax.ShapeDtypeStruct((feats // replicas, width), bf16),
        ),
        in_specs=[hbm] * 3,
        out_specs=(hbm, pl.BlockSpec(memory_space=pltpu.VMEM)),
        scratch_shapes=[
            pltpu.VMEM((PASSES, 16, rows, cols), bf16),
            pltpu.VMEM((tiles, feats, rows), bf16),
            pltpu.VMEM((feats, width), bf16),
            pltpu.VMEM((feats, width), bf16),
            pltpu.VMEM((PASSES, 2, feats, cols), f32),
            pltpu.VMEM((PASSES, feats, cols), f32),
            pltpu.VMEM((PASSES, Z, part, cols), bf16),
            pltpu.VMEM((PASSES, Z, part, cols), bf16),
            pltpu.VMEM((2, part // 2, width), f32),
            pltpu.VMEM((part // 2, width), f32),
            pltpu.VMEM((part // 2, width), f32),
            pltpu.VMEM((tiles, feats, rows), bf16),
            pltpu.SemaphoreType.DMA((PASSES + tiles + 1,)),
            pltpu.SemaphoreType.DMA((96,)),
            pltpu.SemaphoreType.DMA((PASSES, 16, 2)),
            pltpu.SemaphoreType.DMA((2,)),
            pltpu.SemaphoreType.DMA((PASSES,)),
            pltpu.SemaphoreType.DMA((PASSES, Z)),
            pltpu.SemaphoreType.DMA((2,)),
            pltpu.SemaphoreType.REGULAR((2, 6)),
        ],
        compiler_params=pltpu.CompilerParams(collective_id=0, has_side_effects=True),
    )(inputs.T, grad_keys, kv_weight)
    return gi.T, gw


def solution(mesh):
    in_specs = (P(("dp", "col"), "row"), P(("dp", "row"), "col"), P("row", "col"))
    out_specs = (P(("dp", "col"), "row"), P(("row", "dp"), "col"))
    return jax.shard_map(
        per_device, mesh=mesh, in_specs=in_specs, out_specs=out_specs, check_vma=False
    )
```

```python
import functools

import jax
import jax.numpy as jnp
from jax import lax
from jax.experimental import pallas as pl
from jax.experimental.pallas import tpu as pltpu
from jax.sharding import PartitionSpec as P

PROGRAM = [
    ("F", 0), ("F", 1), ("Y", 0), ("D", 0), ("X", 0), ("Y", 1), ("X", 1), ("R", 0), ("Y", 4), ("L", 0), ("X", 4),
    ("T", 1), ("L", 1), ("R", 1), ("Y", 5), ("T", 2), ("X", 5), ("Y", 2), ("X", 2), ("T", 3), ("Y", 3), ("X", 3),
    ("Y", 6), ("T", 4), ("X", 6), ("Y", 7), ("W", 0), ("L", 3), ("T", 5), ("R", 3), ("R", 2), ("L", 2), ("T", 6),
    ("X", 7), ("O", 1), ("R", 4), ("L", 5), ("L", 6), ("O", 0), ("O", 3), ("O", 2), ("C", 0), ("R", 6), ("L", 4),
    ("R", 5), ("R", 7), ("V", 0), ("L", 7), ("Z", 0), ("O", 4), ("O", 5), ("O", 6), ("O", 7), ("C", 1), ("E", 0),
]
MESH = pl.DeviceIdType.MESH
PASSES = 2
LINE = 4
Z = 12


def dot_rows(a, b):
    return lax.dot_general(a, b, (((1,), (0,)), ((), ())), preferred_element_type=jnp.float32)


def dot_last(a, b):
    return lax.dot_general(a, b, (((1,), (1,)), ((), ())), preferred_element_type=jnp.float32)


def kernel(
    norm, xt_hbm, gk_hbm, w_hbm, gi_hbm, gw_out,
    blocks, xs, w_own, w_far, acc, sib, z_send, z_recv, sums, near_in, far_in, gi_tiles,
    local_sem, send_sem, block_sem, w_sem, sib_sem, z_sem, fin_sem, token_sem,
):
    rows, cols = gk_hbm.shape[0], gk_hbm.shape[1] // PASSES
    feats = w_hbm.shape[0]
    part = feats // Z
    dp, row, p = lax.axis_index("dp"), lax.axis_index("row"), lax.axis_index("col")
    z, core = dp // 2, dp % 2
    x, v = row // LINE, row % LINE
    u = (x + LINE - 2 * p) % LINE
    far = u // 2
    sibling = {"dp": 2 * z + 1 - core}
    partner = {"col": 1 - p}
    x_up = {"row": ((x + 1) % LINE) * LINE + v}
    x_down = {"row": ((x + LINE - 1) % LINE) * LINE + v}
    y_up, y_down = {"row": row + 1}, {"row": row - 1}

    started = []
    sends = iter(range(10_000))

    def send(src, dst, recv, device, when=None):
        copy = pltpu.make_async_remote_copy(
            src_ref=src, dst_ref=dst, send_sem=send_sem.at[next(sends)], recv_sem=recv,
            device_id=device, device_id_type=MESH,
        )
        started.append((copy, when))
        if when is None:
            copy.start()
        else:
            pl.when(when)(copy.start)

    def arrived(dst, recv, device, when=None):
        copy = pltpu.make_async_remote_copy(
            src_ref=dst, dst_ref=dst, send_sem=send_sem.at[0], recv_sem=recv,
            device_id=device, device_id_type=MESH,
        )
        if when is None:
            copy.wait_recv()
        else:
            pl.when(when)(copy.wait_recv)

    def order(line_far, k):
        upper = v // 2
        mirrored = v + upper * (3 - 2 * v)
        near_k = (mirrored, 1 - mirrored, 2, 3)[k]
        far_k = (3, 2, 0, 1)[k]
        low = line_far * far_k + (1 - line_far) * near_k
        return low + upper * (3 - 2 * low)

    def column_slot(uu, k):
        ff = uu // 2
        return ff * (20 - 4 * uu) + (1 - ff) * 4 * uu + order(ff, k)

    def half(s, slot, i):
        return blocks.at[s, slot, pl.ds(i * (rows // 2), rows // 2)]

    def accumulate(s, slot):
        h, t = slot // 8, slot % 8
        acc[s, h] += dot_rows(xs[t], blocks[s, slot])

    own_slot = 4 * u + v
    own = [
        pltpu.make_async_copy(gk_hbm.at[:, pl.ds(s * cols, cols)], blocks.at[s, own_slot], local_sem.at[s])
        for s in range(PASSES)
    ]
    tiles = xs.shape[0]
    loads = [
        pltpu.make_async_copy(xt_hbm.at[:, pl.ds(t * rows, rows)], xs.at[t], local_sem.at[PASSES + t])
        for t in range(tiles)
    ]
    load_w = pltpu.make_async_copy(w_hbm, w_own, local_sem.at[PASSES + tiles])
    is_near, is_far = far == 0, far == 1
    for copy in own:
        pl.when(is_near)(copy.start)

    far_u = u - 2
    far_x = (3 - far_u + 2 * (1 - p)) % LINE
    far_entry = 3 * (1 - v // 2)
    far_device = {"row": far_x * LINE + far_entry, "col": 1 - p}
    far_slot = 8 + 4 * far_u + v

    def start_far(s):
        send(
            gk_hbm.at[:, pl.ds(s * cols, cols)], blocks.at[s, far_slot], block_sem.at[s, far_slot, 0],
            far_device, is_far,
        )

    def line_step(s, k):
        j = order(far, k)
        slot = column_slot(u, k)
        here, sem = blocks.at[s, slot], block_sem.at[s, slot, 0]
        entry = far * 3 * (1 - j // 2) + (1 - far) * j
        if k == 0:
            pl.when(is_near)(own[s].wait)
            arrived(here, sem, sibling, is_far)
        else:
            arrived(here, sem, sibling)
        send(here, here, sem, y_down, jnp.logical_and(v <= entry, v > 0))
        send(here, here, sem, y_up, jnp.logical_and(v >= entry, v < LINE - 1))

    def ring_step(s, k):
        slot = column_slot(u, k)
        here, sem = blocks.at[s, slot], block_sem.at[s, slot, 0]
        send(here, here, sem, x_up)
        send(here, here, sem, x_down)
        accumulate(s, slot)

    def left_step(s, k):
        slot = column_slot((u + LINE - 1) % LINE, k)
        arrived(blocks.at[s, slot], block_sem.at[s, slot, 0], sibling)
        send(half(s, slot, 0), half(s, slot, 0), block_sem.at[s, slot, 0], x_up)
        accumulate(s, slot)

    def right_step(s, k):
        slot = column_slot((u + 1) % LINE, k)
        arrived(blocks.at[s, slot], block_sem.at[s, slot, 0], sibling)
        send(half(s, slot, 1), half(s, slot, 1), block_sem.at[s, slot, 1], x_down)
        accumulate(s, slot)

    def opposite_step(s, k):
        slot = column_slot((u + 2) % LINE, k)
        for i in range(2):
            arrived(half(s, slot, i), block_sem.at[s, slot, i], sibling)
        accumulate(s, slot)

    def cores_start(s):
        send(acc.at[s, 1 - core], sib.at[s], sib_sem.at[s], sibling)

    def z_start(s):
        arrived(sib.at[s], sib_sem.at[s], sibling)
        acc[s, core] += sib[s]
        for zz in range(Z):
            z_send[s, zz] = acc[s, core, pl.ds(zz * part, part)].astype(jnp.bfloat16)
        for d in range(1, Z):
            to = (z + d) % Z
            send(z_send.at[s, to], z_recv.at[s, z], z_sem.at[s, z], {"dp": 2 * to + core})

    def z_finish(s):
        total = acc[s, core, pl.ds(pl.multiple_of(z * part, 8), part)]
        for d in range(1, Z):
            source = (z + Z - d) % Z
            arrived(z_recv.at[s, source], z_sem.at[s, source], sibling)
            total = total + z_recv[s, source].astype(jnp.float32)
        for i in range(2):
            sums[i, :, s * cols:(s + 1) * cols] = total[i * (part // 2):(i + 1) * (part // 2)]

    w_rows = feats // 2
    w_part = w_far.at[pl.ds(pl.multiple_of(core * w_rows, 16), w_rows)]
    w_other = w_far.at[pl.ds(pl.multiple_of((1 - core) * w_rows, 16), w_rows)]

    barrier = pltpu.get_barrier_semaphore()

    def greet(device, when=None):
        def signal():
            pl.semaphore_signal(barrier, inc=1, device_id=device, device_id_type=MESH)

        if when is None:
            signal()
        else:
            pl.when(when)(signal)

    greet(x_up)
    greet(x_down)
    greet(sibling)
    for k in range(2):
        greet({"dp": 2 * z + k, "col": 1 - p})
    for step in (1, 7):
        y = (4 * p + v + step) % 8
        greet({"row": x * LINE + y % LINE, "col": y // LINE})
    z_up, z_down = {"dp": 2 * ((z + 1) % Z) + core}, {"dp": 2 * ((z + Z - 1) % Z) + core}
    greet(z_up)
    greet(z_down)
    far_greets = jnp.logical_and(is_far, v % 3 == 0)
    for i in range(2):
        source_x = (5 - u + 2 * (1 - p)) % LINE
        greet({"row": source_x * LINE + 2 * (1 - v // 3) + i, "col": 1 - p}, far_greets)

    for copy in loads:
        copy.start()
    load_w.start()
    acc[...] = jnp.zeros_like(acc)
    pl.semaphore_wait(barrier, 9 + far)
    def wait_loads():
        for copy in loads:
            copy.wait()

    def weight_send():
        send(w_hbm.at[pl.ds(pl.multiple_of(core * w_rows, 16), w_rows)], w_part, w_sem.at[0], partner)

    def weight_forward():
        arrived(w_part, w_sem.at[0], sibling)
        send(w_part, w_part, w_sem.at[1], sibling)

    def token_round(r):
        for i, (device, rounds) in enumerate(((z_up, 5), (z_down, 4))):
            if 1 <= r - 1 <= rounds:
                pl.semaphore_wait(token_sem.at[i, r - 1], 1)
            if r <= rounds:
                pl.semaphore_signal(token_sem.at[i, r], inc=1, device_id=device, device_id_type=MESH)

    steps = dict(
        T=token_round, D=lambda i: wait_loads(),
        F=lambda i: start_far(i), W=lambda i: weight_send(), V=lambda i: weight_forward(),
        Y=lambda i: line_step(*divmod(i, LINE)), X=lambda i: ring_step(*divmod(i, LINE)),
        L=lambda i: left_step(*divmod(i, LINE)), R=lambda i: right_step(*divmod(i, LINE)),
        O=lambda i: opposite_step(*divmod(i, LINE)),
        C=cores_start, Z=z_start, E=z_finish,
    )
    for name, i in PROGRAM:
        steps[name](i)
    load_w.wait()
    arrived(w_other, w_sem.at[1], sibling)
    z_start(1)

    def tile(t, carry):
        def term(weight, slot):
            total = dot_last(weight[:, :cols], blocks[0, slot])
            for s in range(1, PASSES):
                total = total + dot_last(weight[:, s * cols:(s + 1) * cols], blocks[s, slot])
            return total.astype(jnp.bfloat16).astype(jnp.float32)

        gi_tiles[t] = (term(w_own, t) + term(w_far, t + 8)).astype(jnp.bfloat16)
        return carry

    lax.fori_loop(0, tiles, tile, 0)
    stores = [
        pltpu.make_async_copy(gi_tiles.at[t], gi_hbm.at[:, pl.ds(t * rows, rows)], local_sem.at[t])
        for t in range(tiles)
    ]
    for copy in stores:
        copy.start()

    z_finish(1)
    is_zero, is_one = core == 0, core == 1
    send(sums.at[1], near_in, fin_sem.at[0], sibling, is_zero)
    send(sums.at[0], far_in, fin_sem.at[1], {"dp": 2 * z, "col": 1 - p}, is_one)
    send(sums.at[1], far_in, fin_sem.at[1], {"dp": 2 * z + 1, "col": 1 - p}, is_one)

    arrived(far_in, fin_sem.at[1], sibling)

    @pl.when(is_zero)
    def _():
        gw_out[...] = ((sums[0] + far_in[...]) * norm).astype(jnp.bfloat16)

    @pl.when(is_one)
    def _():
        arrived(near_in, fin_sem.at[0], sibling)
        gw_out[...] = ((near_in[...] + far_in[...]) * norm).astype(jnp.bfloat16)

    for copy in stores:
        copy.wait()
    for copy, when in started:
        if when is None:
            copy.wait_send()
        else:
            pl.when(when)(copy.wait_send)


def per_device(inputs, grad_keys, kv_weight):
    tokens, feats = inputs.shape
    rows, width = grad_keys.shape
    cols = width // PASSES
    tiles = tokens // rows
    replicas = lax.axis_size("dp")
    part = feats // Z
    norm = float(tokens * lax.axis_size("col") * replicas) ** (-0.5)
    bf16, f32 = jnp.bfloat16, jnp.float32
    hbm = pl.BlockSpec(memory_space=pl.ANY)
    gi, gw = pl.pallas_call(
        functools.partial(kernel, norm),
        out_shape=(
            jax.ShapeDtypeStruct((feats, tokens), bf16),
            jax.ShapeDtypeStruct((feats // replicas, width), bf16),
        ),
        in_specs=[hbm] * 3,
        out_specs=(hbm, pl.BlockSpec(memory_space=pltpu.VMEM)),
        scratch_shapes=[
            pltpu.VMEM((PASSES, 16, rows, cols), bf16),
            pltpu.VMEM((tiles, feats, rows), bf16),
            pltpu.VMEM((feats, width), bf16),
            pltpu.VMEM((feats, width), bf16),
            pltpu.VMEM((PASSES, 2, feats, cols), f32),
            pltpu.VMEM((PASSES, feats, cols), f32),
            pltpu.VMEM((PASSES, Z, part, cols), bf16),
            pltpu.VMEM((PASSES, Z, part, cols), bf16),
            pltpu.VMEM((2, part // 2, width), f32),
            pltpu.VMEM((part // 2, width), f32),
            pltpu.VMEM((part // 2, width), f32),
            pltpu.VMEM((tiles, feats, rows), bf16),
            pltpu.SemaphoreType.DMA((PASSES + tiles + 1,)),
            pltpu.SemaphoreType.DMA((96,)),
            pltpu.SemaphoreType.DMA((PASSES, 16, 2)),
            pltpu.SemaphoreType.DMA((2,)),
            pltpu.SemaphoreType.DMA((PASSES,)),
            pltpu.SemaphoreType.DMA((PASSES, Z)),
            pltpu.SemaphoreType.DMA((2,)),
            pltpu.SemaphoreType.REGULAR((2, 6)),
        ],
        compiler_params=pltpu.CompilerParams(collective_id=0, has_side_effects=True),
    )(inputs.T, grad_keys, kv_weight)
    return gi.T, gw


def solution(mesh):
    in_specs = (P(("dp", "col"), "row"), P(("dp", "row"), "col"), P("row", "col"))
    out_specs = (P(("dp", "col"), "row"), P(("row", "dp"), "col"))
    return jax.shard_map(
        per_device, mesh=mesh, in_specs=in_specs, out_specs=out_specs, check_vma=False
    )
```
